32 devices in a mesh: dp: 32 (over z, y, x, core).
Axes of the slice: x: 2, y: 2, z: 4, core: 2. Of those that a mesh axis runs over, the one named last changes fastest.
Arguments:
- tokens: bfloat16 [4096, 1088], P('dp'), may hold values from -6 to 6
- params: bfloat16 [14221312], P('dp'), may hold values from -2 to 2, as said below
- lengths: int32 [64], P('dp'), may hold values from 1 to 64, as said below
- cotangent: bfloat16 [4096, 1088], P('dp'), may hold values from -6 to 6
Outputs:
- block_out: float32 [4096, 1088], P('dp')
- token_grad: float32 [4096, 1088], P('dp')
- param_grad: float32 [14221312], P('dp')
The draws below stay inside these ranges and needn't reach their ends.
Inputs may be any that keep to these rules, and one draw needn't show every extreme that they name: Each sequence's valid tokens are its first lengths slots; some sequence fills all 64. `params`: entries from 14217984 on are zero.
All inputs are finite; a program needn't handle non-finite values.
Results may differ from the reference program's by a relative error of at most 0.0084.
Values may be sent and summed in bfloat16 or wider, within the bound.
No kernel may reach another device: no remote copies, remote signals or barrier semaphores. Data moves between devices by JAX's collectives and lax.ppermute only.
A program may use at most 256 MiB of HBM per device.

```python
import math
import jax
import jax.numpy as jnp
from jax import lax

HEADS = 17
HEAD = 64
D = 1088
FF = 4352
SLOT = 64
NSEQ = 64
TOKENS = 4096
P_SIZE = 14217984
P_PAD = 14221312


def draw_params(key, part):
    width = HEADS * HEAD
    keys = jax.random.split(key, 16)

    def normal_piece(index, layout, scale):
        return scale * jax.random.truncated_normal(keys[index], -3.0, 3.0, layout, jnp.float32)
    first_norm_gain = jax.random.uniform(keys[0], (width,), jnp.float32, 0.6, 1.4)
    second_norm_gain = jax.random.uniform(keys[7], (width,), jnp.float32, 0.6, 1.4)
    bias_scale = 0.3
    w_query = normal_piece(2, (width, width), 1.0 / math.sqrt(width))
    w_key = normal_piece(13, (width, width), 1.0 / math.sqrt(width))
    w_value = normal_piece(14, (width, width), 1.0 / math.sqrt(width))
    w_qkv = jnp.concatenate([w_query, w_key, w_value], axis=1)
    pieces = [first_norm_gain, normal_piece(1, (width,), bias_scale), w_qkv, normal_piece(3, (width,), bias_scale), normal_piece(4, (width,), bias_scale), normal_piece(5, (width, width), math.sqrt(max(SLOT / 4.0, 1.0)) / math.sqrt(width)), normal_piece(6, (width,), bias_scale), second_norm_gain, normal_piece(8, (width,), bias_scale), normal_piece(9, (width, FF), 1.0 / math.sqrt(width)), normal_piece(10, (FF,), bias_scale), normal_piece(11, (FF, width), 1.5 / math.sqrt(FF)), normal_piece(12, (width,), bias_scale)]
    flat = jnp.concatenate([piece.reshape(-1) for piece in pieces])
    return jnp.concatenate([flat, jnp.zeros((P_PAD - P_SIZE,), jnp.float32)]).astype(jnp.bfloat16)


def draw_lengths(key, part):
    first, second = jax.random.split(key)
    lengths = jax.random.randint(first, (NSEQ,), 1, SLOT + 1, dtype=jnp.int32)
    where = jax.random.randint(second, (), 0, NSEQ, dtype=jnp.int32)
    return lengths.at[where].set(SLOT)


def level_of(key, shape, cuts, smallest, largest):
    loudness = 1.0
    for axis_at, parts in cuts:
        heights = jax.random.uniform(jax.random.fold_in(jax.random.fold_in(key, 6), axis_at), (parts,), jnp.float32, smallest / len(cuts), largest / len(cuts))
        loudness = loudness * jnp.repeat(jnp.exp(heights), shape[axis_at] // parts).reshape((-1,) + (1,) * (len(shape) - 1 - axis_at))
    return loudness


def bell_draw(key, shape, spread, bound, cuts=(), held_as=jnp.bfloat16):
    array = spread * jax.random.normal(key, shape, jnp.float32)
    if cuts:
        array = array * level_of(key, shape, cuts, -0.22, 0.18)
    return jnp.clip(array, -bound, bound).astype(held_as)


def setup_inputs(seed: int = 0) -> dict:
    seeds = jax.random.split(jax.random.key(seed), 5)
    tokens = bell_draw(seeds[0], (TOKENS, D), 1.0, 6.0, ((0, 32),))
    params = draw_params(jax.random.fold_in(seeds[4], 71), 0)
    lengths = draw_lengths(jax.random.fold_in(seeds[4], 71), 0)
    cotangent = bell_draw(seeds[3], (TOKENS, D), 1.0, 6.0, ((0, 32),))
    return dict(tokens=tokens, params=params, lengths=lengths, cotangent=cotangent)


EPS = 1e-05
NEGATIVE = -1e+30
GELU_C = 0.7978845608028654

def param_shapes(width, hidden):
    return [(width,), (width,), (width, 3 * width), (width,), (width,), (width, width), (width,), (width,), (width,), (width, hidden), (hidden,), (hidden, width), (width,)]

def unflatten(flat, width, hidden):
    pieces = []
    offset = 0
    for layout in param_shapes(width, hidden):
        extent = math.prod(layout)
        pieces.append(flat[offset:offset + extent].reshape(layout))
        offset += extent
    return pieces

def batched(form, left, right):
    return jnp.einsum(form, left.astype(jnp.float32), right.astype(jnp.float32))

def matmul(left, right):
    return jnp.dot(left, right, preferred_element_type=jnp.float32)

def contract_rows(left, right):
    return lax.dot_general(left, right, (((0,), (0,)), ((), ())), preferred_element_type=jnp.float32)

def contract_cols(left, right):
    return lax.dot_general(left, right, (((1,), (1,)), ((), ())), preferred_element_type=jnp.float32)

def layer_norm_forward(rows, gain, shift):
    mean = lax.optimization_barrier(jnp.mean(rows, axis=-1, keepdims=True))
    centred = rows - mean
    inverse = lax.rsqrt(lax.optimization_barrier(jnp.mean(centred * centred, axis=-1, keepdims=True)) + EPS)
    normed = centred * inverse
    return (normed * gain.astype(jnp.float32) + shift.astype(jnp.float32), normed, inverse)

def layer_norm_backward(upstream, normed, inverse, gain):
    dgain = lax.optimization_barrier(jnp.sum(upstream * normed, axis=0))
    dshift = lax.optimization_barrier(jnp.sum(upstream, axis=0))
    scaled = upstream * gain.astype(jnp.float32)
    inner = scaled - lax.optimization_barrier(jnp.mean(scaled, axis=-1, keepdims=True)) - normed * lax.optimization_barrier(jnp.mean(scaled * normed, axis=-1, keepdims=True))
    return (dgain, dshift, inverse * inner)

def gelu(value):
    return 0.5 * value * (1.0 + jnp.tanh(GELU_C * (value + 0.044715 * value * value * value)))

def attention_mask(lengths, slots):
    position = jnp.arange(slots, dtype=jnp.int32)
    causal = position[:, None] >= position[None, :]
    inside = position[None, None, :] < lengths.astype(jnp.int32)[:, None, None]
    return (causal[None, :, :] & inside)[:, None, :, :]

def row_valid(lengths, slots):
    position = jnp.arange(slots, dtype=jnp.int32)
    return (position[None, :] < lengths.astype(jnp.int32)[:, None]).astype(jnp.float32).reshape(-1, 1)

def split_heads(block, seqs, slots):
    return block.reshape(seqs, slots, HEADS, HEAD)

def raw_scores(queries, key_rows, sequence_mask):
    scores = batched('gqhd,gkhd->ghqk', queries, key_rows) * (1.0 / math.sqrt(HEAD))
    return jnp.where(sequence_mask, scores, NEGATIVE)

def forward_pass(weights, tokens, lengths):
    first_norm_gain, first_norm_shift, w_qkv, bias_q, bias_v, w_out, bias_out, second_norm_gain, second_norm_shift, w_up, bias_up, w_down, bias_down = weights
    width = tokens.shape[1]
    seqs = lengths.shape[0]
    slots = tokens.shape[0] // seqs
    sequence_mask = attention_mask(lengths, slots)
    token_valid_mask = row_valid(lengths, slots)
    residual_stream = tokens.astype(jnp.float32)
    first_centred_scaled, first_standardized_input, first_inverse_deviation = layer_norm_forward(residual_stream, first_norm_gain, first_norm_shift)
    first_norm_output = first_centred_scaled.astype(jnp.bfloat16)
    qkv_bias = jnp.concatenate([bias_q.astype(jnp.float32), jnp.zeros((width,), jnp.float32), bias_v.astype(jnp.float32)])
    query_key_value = (matmul(first_norm_output, w_qkv) + qkv_bias).astype(jnp.bfloat16)
    queries = split_heads(query_key_value[:, :width], seqs, slots)
    key_rows = split_heads(query_key_value[:, width:2 * width], seqs, slots)
    values = split_heads(query_key_value[:, 2 * width:], seqs, slots)
    scores = raw_scores(queries, key_rows, sequence_mask)
    peak = lax.optimization_barrier(jnp.max(scores, axis=-1, keepdims=True))
    log_exp_totals = peak + jnp.log(lax.optimization_barrier(jnp.sum(jnp.exp(scores - peak), axis=-1, keepdims=True)))
    probs = jnp.exp(scores - log_exp_totals).astype(jnp.bfloat16)
    attention_result = batched('ghqk,gkhd->gqhd', probs, values).astype(jnp.bfloat16).reshape(-1, width)
    middle_residual = residual_stream + matmul(attention_result, w_out) + bias_out.astype(jnp.float32)
    second_centred_scaled, second_standardized_input, second_inverse_deviation = layer_norm_forward(middle_residual, second_norm_gain, second_norm_shift)
    second_norm_output = second_centred_scaled.astype(jnp.bfloat16)
    preactivation_values = matmul(second_norm_output, w_up) + bias_up.astype(jnp.float32)
    activation_values = gelu(preactivation_values).astype(jnp.bfloat16)
    block_out = token_valid_mask * (middle_residual + matmul(activation_values, w_down) + bias_down.astype(jnp.float32))
    stored_forward_values = (token_valid_mask, sequence_mask, first_standardized_input, first_inverse_deviation, first_norm_output, query_key_value, log_exp_totals, attention_result, second_standardized_input, second_inverse_deviation, second_norm_output, preactivation_values, activation_values)
    return (stored_forward_values, block_out)

def backward_pass(weights, stored_forward_values, cotangent, lengths):
    first_norm_gain, first_norm_shift, w_qkv, bias_q, bias_v, w_out, bias_out, second_norm_gain, second_norm_shift, w_up, bias_up, w_down, bias_down = weights
    token_valid_mask, sequence_mask, first_standardized_input, first_inverse_deviation, first_norm_output, query_key_value, log_exp_totals, attention_result, second_standardized_input, second_inverse_deviation, second_norm_output, preactivation_values, activation_values = stored_forward_values
    width = cotangent.shape[1]
    seqs = lengths.shape[0]
    slots = cotangent.shape[0] // seqs
    dout = token_valid_mask * cotangent.astype(jnp.float32)
    dout_b = dout.astype(jnp.bfloat16)
    grad_down = contract_rows(activation_values, dout_b)
    grad_bias_down = lax.optimization_barrier(jnp.sum(dout, axis=0))
    dact = contract_cols(dout_b, w_down)
    dpre = jax.vjp(gelu, preactivation_values)[1](dact)[0]
    dpre_b = dpre.astype(jnp.bfloat16)
    grad_up = contract_rows(second_norm_output, dpre_b)
    grad_bias_up = lax.optimization_barrier(jnp.sum(dpre, axis=0))
    second_norm_input_gradient = contract_cols(dpre_b, w_up)
    second_gain_gradient, second_shift_gradient, second_normed_gradient = layer_norm_backward(second_norm_input_gradient, second_standardized_input, second_inverse_deviation, second_norm_gain)
    dmid = dout + second_normed_gradient
    dmid_b = dmid.astype(jnp.bfloat16)
    grad_out = contract_rows(attention_result, dmid_b)
    grad_bias_out = lax.optimization_barrier(jnp.sum(dmid, axis=0))
    dattn = contract_cols(dmid_b, w_out).astype(jnp.bfloat16)
    queries = split_heads(query_key_value[:, :width], seqs, slots)
    key_rows = split_heads(query_key_value[:, width:2 * width], seqs, slots)
    values = split_heads(query_key_value[:, 2 * width:], seqs, slots)
    scores = raw_scores(queries, key_rows, sequence_mask)
    probs_full = jnp.exp(scores - log_exp_totals)
    probs = probs_full.astype(jnp.bfloat16)
    dattn_heads = split_heads(dattn, seqs, slots)
    dprobs = batched('gqhd,gkhd->ghqk', dattn_heads, values)
    dscores = probs_full * (dprobs - lax.optimization_barrier(jnp.sum(probs_full * dprobs, axis=-1, keepdims=True)))
    dscores_b = dscores.astype(jnp.bfloat16)
    factor = 1.0 / math.sqrt(HEAD)
    dquery = (batched('ghqk,gkhd->gqhd', dscores_b, key_rows) * factor).reshape(-1, width)
    dkey = (batched('ghqk,gqhd->gkhd', dscores_b, queries) * factor).reshape(-1, width)
    dvalue = batched('ghqk,gqhd->gkhd', probs, dattn_heads).reshape(-1, width)
    grad_bias_q = lax.optimization_barrier(jnp.sum(dquery, axis=0))
    grad_bias_v = lax.optimization_barrier(jnp.sum(dvalue, axis=0))
    dqkv = jnp.concatenate([dquery, dkey, dvalue], axis=1).astype(jnp.bfloat16)
    grad_qkv = contract_rows(first_norm_output, dqkv)
    first_norm_input_gradient = contract_cols(dqkv, w_qkv)
    first_gain_gradient, first_shift_gradient, first_normed_gradient = layer_norm_backward(first_norm_input_gradient, first_standardized_input, first_inverse_deviation, first_norm_gain)
    token_grad = dmid + first_normed_gradient
    grads = [first_gain_gradient, first_shift_gradient, grad_qkv, grad_bias_q, grad_bias_v, grad_out, grad_bias_out, second_gain_gradient, second_shift_gradient, grad_up, grad_bias_up, grad_down, grad_bias_down]
    return (token_grad, grads)

def reference(tokens, params, lengths, cotangent):
    width = HEADS * HEAD
    weights = unflatten(params, width, FF)
    groups = NSEQ // 32
    group_rows = 32 * SLOT
    token_blocks = tokens.reshape(groups, group_rows, width)
    length_blocks = lengths.reshape(groups, 32)
    cot_blocks = cotangent.reshape(groups, group_rows, width)

    def advance(carry, item):
        part_tokens, part_lengths, part_cot = item
        stored_forward_values, block_out = forward_pass(weights, part_tokens, part_lengths)
        token_grad, grads = backward_pass(weights, stored_forward_values, part_cot, part_lengths)
        return ([total + piece for total, piece in zip(carry, grads)], (block_out, token_grad))
    start = [jnp.zeros(layout, jnp.float32) for layout in param_shapes(width, FF)]
    totals, (outputs, token_grads) = lax.scan(advance, start, (token_blocks, length_blocks, cot_blocks))
    flat = jnp.concatenate([piece.reshape(-1) for piece in totals])
    flat = jnp.concatenate([flat, jnp.zeros((P_PAD - P_SIZE,), jnp.float32)])
    return (outputs.reshape(TOKENS, width), token_grads.reshape(TOKENS, width), flat)
```

```python
import math

import jax
import jax.numpy as jnp
from jax import lax
from jax.experimental import pallas as pl
from jax.experimental.pallas import tpu as pltpu
from jax.sharding import PartitionSpec as P

HEADS = 17
HEAD = 64
FF = 4352


EPS = 1e-05
NEGATIVE = -1e30
GELU_C = 0.7978845608028654


def swapped(block, axis, stride):
    count = lax.axis_size(axis)
    route = []
    for low in range(count):
        high = low | 1 << stride
        if high != low and high < count:
            route += [(low, high), (high, low)]
    return lax.ppermute(block, axis, route)


def param_shapes(width, hidden):
    return [
        (width,),
        (width,),
        (width, 3 * width),
        (width,),
        (width,),
        (width, width),
        (width,),
        (width,),
        (width,),
        (width, hidden),
        (hidden,),
        (hidden, width),
        (width,),
    ]


def unflatten(flat, width, hidden):
    pieces = []
    offset = 0
    for layout in param_shapes(width, hidden):
        extent = math.prod(layout)
        pieces.append(flat[offset : offset + extent].reshape(layout))
        offset += extent
    return pieces


def batched(form, left, right):
    return jnp.einsum(form, left, right, preferred_element_type=jnp.float32)


def matmul(left, right):
    return jnp.dot(left, right, preferred_element_type=jnp.float32)


def contract_rows(left, right):
    return lax.dot_general(
        left, right, (((0,), (0,)), ((), ())), preferred_element_type=jnp.float32
    )


def contract_cols(left, right):
    return lax.dot_general(
        left, right, (((1,), (1,)), ((), ())), preferred_element_type=jnp.float32
    )


def layer_norm_forward(rows, gain, shift):
    mean = jnp.mean(rows, axis=-1, keepdims=True)
    centred = rows - mean
    inverse = lax.rsqrt(jnp.mean(centred * centred, axis=-1, keepdims=True) + EPS)
    normed = centred * inverse
    return (normed * gain.astype(jnp.float32) + shift.astype(jnp.float32), normed, inverse)


def layer_norm_backward(upstream, normed, inverse, gain):
    dgain = jnp.sum(upstream * normed, axis=0)
    dshift = jnp.sum(upstream, axis=0)
    scaled = upstream * gain.astype(jnp.float32)
    inner = (
        scaled
        - jnp.mean(scaled, axis=-1, keepdims=True)
        - normed * jnp.mean(scaled * normed, axis=-1, keepdims=True)
    )
    return (dgain, dshift, inverse * inner)


def gelu(value):
    return 0.5 * value * (1.0 + jnp.tanh(GELU_C * (value + 0.044715 * value * value * value)))


def attention_mask(lengths, slots):
    position = jnp.arange(slots, dtype=jnp.int32)
    causal = position[:, None] >= position[None, :]
    inside = position[None, None, :] < lengths[:, None, None]
    return (causal[None, :, :] & inside)[:, None, :, :]


def row_valid(lengths, slots):
    position = jnp.arange(slots, dtype=jnp.int32)
    return (position[None, :] < lengths[:, None]).astype(jnp.float32).reshape(-1, 1)


def split_heads(block, seqs, slots):
    return block.reshape(seqs, slots, HEADS, HEAD)


def raw_scores(queries, key_rows, sequence_mask):
    scores = batched("gqhd,gkhd->ghqk", queries, key_rows) * (1.0 / math.sqrt(HEAD))
    return jnp.where(sequence_mask, scores, NEGATIVE)


def forward_pass(weights, tokens, lengths):
    (
        first_norm_gain,
        first_norm_shift,
        w_qkv,
        bias_q,
        bias_v,
        w_out,
        bias_out,
        second_norm_gain,
        second_norm_shift,
        w_up,
        bias_up,
        w_down,
        bias_down,
    ) = weights
    width = tokens.shape[1]
    seqs = lengths.shape[0]
    slots = tokens.shape[0] // seqs
    sequence_mask = attention_mask(lengths, slots)
    token_valid_mask = row_valid(lengths, slots)
    residual_stream = tokens.astype(jnp.float32)
    first_centred_scaled, first_standardized_input, first_inverse_deviation = layer_norm_forward(
        residual_stream, first_norm_gain, first_norm_shift
    )
    first_norm_output = first_centred_scaled.astype(jnp.bfloat16)
    qkv_bias = jnp.concatenate(
        [bias_q.astype(jnp.float32), jnp.zeros((width,), jnp.float32), bias_v.astype(jnp.float32)]
    )
    query_key_value = (matmul(first_norm_output, w_qkv) + qkv_bias).astype(jnp.bfloat16)
    queries = split_heads(query_key_value[:, :width], seqs, slots)
    key_rows = split_heads(query_key_value[:, width : 2 * width], seqs, slots)
    values = split_heads(query_key_value[:, 2 * width :], seqs, slots)
    scores = raw_scores(queries, key_rows, sequence_mask)
    peak = jnp.max(scores, axis=-1, keepdims=True)
    log_exp_totals = peak + jnp.log(jnp.sum(jnp.exp(scores - peak), axis=-1, keepdims=True))
    probs = jnp.exp(scores - log_exp_totals).astype(jnp.bfloat16)
    attention_result = (
        batched("ghqk,gkhd->gqhd", probs, values).astype(jnp.bfloat16).reshape(-1, width)
    )
    middle_residual = (
        residual_stream + matmul(attention_result, w_out) + bias_out.astype(jnp.float32)
    )
    second_centred_scaled, second_standardized_input, second_inverse_deviation = layer_norm_forward(
        middle_residual, second_norm_gain, second_norm_shift
    )
    second_norm_output = second_centred_scaled.astype(jnp.bfloat16)
    preactivation_values = matmul(second_norm_output, w_up) + bias_up.astype(jnp.float32)
    activation_values = gelu(preactivation_values).astype(jnp.bfloat16)
    block_out = token_valid_mask * (
        middle_residual + matmul(activation_values, w_down) + bias_down.astype(jnp.float32)
    )
    stored_forward_values = (
        token_valid_mask,
        sequence_mask,
        first_standardized_input,
        first_inverse_deviation,
        first_norm_output,
        query_key_value,
        log_exp_totals,
        attention_result,
        second_standardized_input,
        second_inverse_deviation,
        second_norm_output,
        preactivation_values,
        activation_values,
    )
    return (stored_forward_values, block_out)


def backward_pass(weights, stored_forward_values, cotangent, lengths):
    (
        first_norm_gain,
        first_norm_shift,
        w_qkv,
        bias_q,
        bias_v,
        w_out,
        bias_out,
        second_norm_gain,
        second_norm_shift,
        w_up,
        bias_up,
        w_down,
        bias_down,
    ) = weights
    (
        token_valid_mask,
        sequence_mask,
        first_standardized_input,
        first_inverse_deviation,
        first_norm_output,
        query_key_value,
        log_exp_totals,
        attention_result,
        second_standardized_input,
        second_inverse_deviation,
        second_norm_output,
        preactivation_values,
        activation_values,
    ) = stored_forward_values
    width = cotangent.shape[1]
    seqs = lengths.shape[0]
    slots = cotangent.shape[0] // seqs
    dout = token_valid_mask * cotangent.astype(jnp.float32)
    dout_b = dout.astype(jnp.bfloat16)
    grad_down = contract_rows(activation_values, dout_b)
    grad_bias_down = jnp.sum(dout, axis=0)
    dact = contract_cols(dout_b, w_down)
    dpre = jax.vjp(gelu, preactivation_values)[1](dact)[0]
    dpre_b = dpre.astype(jnp.bfloat16)
    grad_up = contract_rows(second_norm_output, dpre_b)
    grad_bias_up = jnp.sum(dpre, axis=0)
    second_norm_input_gradient = contract_cols(dpre_b, w_up)
    second_gain_gradient, second_shift_gradient, second_normed_gradient = layer_norm_backward(
        second_norm_input_gradient,
        second_standardized_input,
        second_inverse_deviation,
        second_norm_gain,
    )
    dmid = dout + second_normed_gradient
    dmid_b = dmid.astype(jnp.bfloat16)
    grad_out = contract_rows(attention_result, dmid_b)
    grad_bias_out = jnp.sum(dmid, axis=0)
    dattn = contract_cols(dmid_b, w_out).astype(jnp.bfloat16)
    queries = split_heads(query_key_value[:, :width], seqs, slots)
    key_rows = split_heads(query_key_value[:, width : 2 * width], seqs, slots)
    values = split_heads(query_key_value[:, 2 * width :], seqs, slots)
    scores = raw_scores(queries, key_rows, sequence_mask)
    probs_full = jnp.exp(scores - log_exp_totals)
    probs = probs_full.astype(jnp.bfloat16)
    dattn_heads = split_heads(dattn, seqs, slots)
    dprobs = batched("gqhd,gkhd->ghqk", dattn_heads, values)
    dscores = probs_full * (dprobs - jnp.sum(probs_full * dprobs, axis=-1, keepdims=True))
    dscores_b = dscores.astype(jnp.bfloat16)
    factor = 1.0 / math.sqrt(HEAD)
    dquery = (batched("ghqk,gkhd->gqhd", dscores_b, key_rows) * factor).reshape(-1, width)
    dkey = (batched("ghqk,gqhd->gkhd", dscores_b, queries) * factor).reshape(-1, width)
    dvalue = batched("ghqk,gqhd->gkhd", probs, dattn_heads).reshape(-1, width)
    grad_bias_q = jnp.sum(dquery, axis=0)
    grad_bias_v = jnp.sum(dvalue, axis=0)
    dqkv = jnp.concatenate([dquery, dkey, dvalue], axis=1).astype(jnp.bfloat16)
    grad_qkv = contract_rows(first_norm_output, dqkv)
    first_norm_input_gradient = contract_cols(dqkv, w_qkv)
    first_gain_gradient, first_shift_gradient, first_normed_gradient = layer_norm_backward(
        first_norm_input_gradient,
        first_standardized_input,
        first_inverse_deviation,
        first_norm_gain,
    )
    token_grad = dmid + first_normed_gradient
    grads = [
        first_gain_gradient,
        first_shift_gradient,
        grad_qkv,
        grad_bias_q,
        grad_bias_v,
        grad_out,
        grad_bias_out,
        second_gain_gradient,
        second_shift_gradient,
        grad_up,
        grad_bias_up,
        grad_down,
        grad_bias_down,
    ]
    return (token_grad, grads)


def flatten_grads(grads, padded_total):
    used = sum((math.prod(piece.shape) for piece in grads))
    tail = jnp.zeros((padded_total - used,), jnp.float32)
    return jnp.concatenate([piece.reshape(-1) for piece in grads] + [tail])


def owner_sum(flat, shard):
    levels = lax.axis_size("dp").bit_length() - 1
    current = flat.reshape((2,) * levels + (shard,))
    remaining = list(range(levels - 1, -1, -1))
    mine = lax.axis_index("dp")
    order = list(range(levels))
    for bit in order:
        where = remaining.index(bit)
        own_bit = mine >> bit & 1
        keep = lax.dynamic_index_in_dim(current, own_bit, where, keepdims=False)
        outgoing = lax.dynamic_index_in_dim(current, 1 - own_bit, where, keepdims=False)
        current = keep + swapped(outgoing, "dp", bit)
        remaining.pop(where)
    return current


LANES = 128
HALF = 64
TILE = 16
QUARTERS = 4
TAIL = 48
MARGIN = 1120
VMEM_BYTES = 60 * 1024 * 1024


def pieces_of(width, hidden):
    short, wide, long = width // HALF, 3 * width // HALF, hidden // HALF
    table = {}
    at = 0
    for name, run, rows in (
        ("norm1", short, 2),
        ("qkv", wide, width),
        ("bias_qv", short, 2),
        ("out", short, width),
        ("norm2", short, 3),
        ("up", long, width),
        ("bias_up", long, 1),
        ("down", short, hidden),
        ("bias_down", short, 1),
    ):
        table[name] = (at, run, rows)
        at += run * rows
    return table


def quarter_plan(width, hidden, half_blocks):
    span = half_blocks // QUARTERS
    plan = [[] for _ in range(QUARTERS)]
    for name, (at, run, rows) in pieces_of(width, hidden).items():
        row = 0
        while row < rows:
            quarter = (at + (row + 1) * run - 1) // span
            last = min(rows, ((quarter + 1) * span - at) // run)
            plan[quarter].append((name, row, last - row))
            row = last
    return plan


def fits(width, hidden, total, devices):
    if devices != 32 or total % (LANES * TILE * devices) or width % HALF or hidden % HALF:
        return False
    for rows in quarter_plan(width, hidden, total // HALF):
        for name, _, count in rows:
            if name in ("qkv", "out", "up", "down") and count % TILE:
                return False
    return True


def unpack_quarter(whole, quarter, width, hidden):
    table = pieces_of(width, hidden)
    rows_q = whole.shape[0] // QUARTERS
    plan = quarter_plan(width, hidden, 2 * whole.shape[0])[quarter]
    base = 2 * (quarter * rows_q - TAIL)
    matrices = ("qkv", "out", "up", "down")
    shapes = []
    for name, _, count in plan:
        run = table[name][1]
        if name in matrices:
            shapes.append(jax.ShapeDtypeStruct((count, run * HALF), jnp.bfloat16))
        else:
            shapes.append(jax.ShapeDtypeStruct((TILE, run * HALF), jnp.float32))
    first = 0 if quarter else TAIL

    def kernel(src, *rest):
        outs = rest[: len(shapes)]
        flat, wide, sem = rest[len(shapes) :]
        copy = pltpu.make_async_copy(
            src.at[pl.ds(quarter * rows_q - TAIL + first, rows_q + TAIL - first)],
            flat.at[pl.ds(first, rows_q + TAIL - first)],
            sem,
        )
        copy.start()
        copy.wait()
        unroll = 7

        def spread(i, _):
            for u in range(unroll):
                step = i * unroll + u
                block = flat[pl.ds(pl.multiple_of(step * TILE, TILE), TILE), :].astype(jnp.float32)
                wide[pl.ds(2 * TILE * step, TILE, stride=2), :] = block
                wide[pl.ds(2 * TILE * step + 1, TILE, stride=2), :] = pltpu.roll(block, HALF, 1)
            return 0

        steps = (rows_q + TAIL) // TILE
        lax.fori_loop(0, steps // unroll, spread, 0)
        for step in range(steps // unroll * unroll, steps):
            block = flat[step * TILE : (step + 1) * TILE, :].astype(jnp.float32)
            wide[pl.ds(2 * TILE * step, TILE, stride=2), :] = block
            wide[pl.ds(2 * TILE * step + 1, TILE, stride=2), :] = pltpu.roll(block, HALF, 1)
        lane = lax.broadcasted_iota(jnp.int32, (TILE, LANES), 1)
        line = lax.broadcasted_iota(jnp.int32, (TILE, LANES), 0)
        for (name, row, count), out in zip(plan, outs):
            at, run, _ = table[name]
            start = at + row * run - base
            odd = (start + run * line) % 2 == 1
            swap = odd & (lane >= HALF)

            def group(g, _, out=out, run=run, start=start, swap=swap):
                begin = start + g * (TILE * run)
                where = pl.ds(pl.multiple_of(g * TILE, TILE), TILE)
                now = wide[pl.ds(begin, TILE, stride=run), :]
                for j in range((run + 1) // 2):
                    if 2 * j + 1 == run:
                        out[where, 2 * j * HALF : run * HALF] = now[:, :HALF].astype(out.dtype)
                        break
                    after = wide[pl.ds(begin + 2 * j + 2, TILE, stride=run), :]
                    value = jnp.where(swap, after, now)
                    out[where, 2 * j * HALF : 2 * j * HALF + LANES] = value.astype(out.dtype)
                    now = after
                return 0

            if name in matrices:
                lax.fori_loop(0, count // TILE, group, 0)
            else:
                group(0, 0)

    outs = pl.pallas_call(
        kernel,
        out_shape=shapes,
        in_specs=[pl.BlockSpec(memory_space=pl.ANY)],
        out_specs=[pl.BlockSpec(memory_space=pltpu.VMEM)] * len(shapes),
        scratch_shapes=[
            pltpu.VMEM((rows_q + TAIL, LANES), jnp.bfloat16),
            pltpu.VMEM((2 * (rows_q + TAIL) + MARGIN, LANES), jnp.float32),
            pltpu.SemaphoreType.DMA,
        ],
        compiler_params=pltpu.CompilerParams(vmem_limit_bytes=VMEM_BYTES),
        name=f"unpack_{quarter}",
    )(whole)
    return {(name, row): out for (name, row, _), out in zip(plan, outs)}


def lane_pad(block):
    return jnp.pad(block, ((0, 0), (0, -block.shape[1] % LANES)))


def vector_rows(rows, run):
    block = jnp.stack(rows).astype(jnp.bfloat16)
    return jnp.pad(block, ((0, TILE - len(rows)), (0, -block.shape[1] % LANES)))


def pack_quarter(grads, quarter, width, hidden, rows_all):
    table = pieces_of(width, hidden)
    rows_q = rows_all // QUARTERS
    shard = rows_q // 8
    base = 2 * rows_q * quarter
    span = 2 * rows_q
    shift = 2 * TAIL
    jobs = []
    for name, (at, run, rows) in table.items():
        for (key, first), block in grads.items():
            if key != name:
                continue
            count = block.shape[0] if name in ("qkv", "out", "up", "down") else TILE
            start = at + first * run - base
            if start >= span or start + min(count, rows) * run <= 0:
                continue
            if start + shift < 0:
                continue
            groups = min(count // TILE, -(-(span - start) // (TILE * run)))
            jobs.append((start + shift, run, groups, block[: groups * TILE]))
    jobs.sort(key=lambda job: job[0])

    def kernel(me_ref, *rest):
        ins = rest[: len(jobs)]
        keep, send = rest[len(jobs) : len(jobs) + 2]
        wide, flat, sems = rest[len(jobs) + 2 :]
        for (start, run, groups, _), src in zip(jobs, ins):

            def group(g, _, src=src, run=run, start=start):
                begin = start + g * (TILE * run)
                where = pl.ds(pl.multiple_of(g * TILE, TILE), TILE)
                for j in range((run + 1) // 2):
                    value = src[where, j * LANES : (j + 1) * LANES].astype(jnp.float32)
                    wide[pl.ds(begin + 2 * j, TILE, stride=run), :] = value
                    if 2 * j + 1 < run:
                        wide[pl.ds(begin + 2 * j + 1, TILE, stride=run), :] = pltpu.roll(value, HALF, 1)
                return 0

            lax.fori_loop(0, groups, group, 0)
        lane = lax.broadcasted_iota(jnp.int32, (TILE, LANES), 1)
        unroll = 7
        me = me_ref[0]
        for rel in range(8):
            where = jnp.bitwise_xor(me, rel) * shard

            def gather(i, _, where=where):
                for u in range(unroll):
                    line = pl.multiple_of(where + (i * unroll + u) * TILE, TILE)
                    low = wide[pl.ds(shift + 2 * line, TILE, stride=2), :]
                    high = wide[pl.ds(shift + 2 * line + 1, TILE, stride=2), :]
                    value = jnp.where(lane < HALF, low, pltpu.roll(high, HALF, 1))
                    flat[pl.ds(line, TILE), :] = value.astype(jnp.bfloat16)
                return 0

            lax.fori_loop(0, shard // TILE // unroll, gather, 0)
            target = send if rel % 2 else keep
            pltpu.make_async_copy(
                flat.at[pl.ds(pl.multiple_of(where, TILE), shard)], target.at[rel // 2], sems.at[rel]
            ).start()
        for rel in range(8):
            target = send if rel % 2 else keep
            pltpu.make_async_copy(
                flat.at[pl.ds(0, shard)], target.at[rel // 2], sems.at[rel]
            ).wait()

    me = (lax.axis_index("dp") % 8).astype(jnp.int32).reshape(1)
    out = jax.ShapeDtypeStruct((4, shard, LANES), jnp.bfloat16)
    return pl.pallas_call(
        kernel,
        out_shape=[out, out],
        in_specs=[pl.BlockSpec(memory_space=pltpu.SMEM)]
        + [pl.BlockSpec(memory_space=pltpu.VMEM)] * len(jobs),
        out_specs=[pl.BlockSpec(memory_space=pl.ANY)] * 2,
        scratch_shapes=[
            pltpu.VMEM((shift + span + MARGIN, LANES), jnp.float32),
            pltpu.VMEM((rows_q, LANES), jnp.bfloat16),
            pltpu.SemaphoreType.DMA((8,)),
        ],
        compiler_params=pltpu.CompilerParams(vmem_limit_bytes=VMEM_BYTES),
        name=f"pack_{quarter}",
    )(me, *[job[3] for job in jobs])


def flipped(block, bit):
    return swapped(block, "dp", bit)


def plane_moved(block, moves):
    route = [(8 * a + i, 8 * b + i) for a, b in moves for i in range(8)]
    return lax.ppermute(block, "dp", route)


def reduce_quarter(keep, send, quarter):
    f32, bf16 = jnp.float32, jnp.bfloat16
    cut = keep.shape[1] // 2 // TILE * TILE
    other = flipped(send, 0)

    def both(i, rows=slice(None)):
        return keep[i, rows].astype(f32) + other[i, rows].astype(f32)

    low, high = slice(0, cut), slice(cut, None)
    diag_x = flipped(both(3, low).astype(bf16), 1)
    diag_y = flipped(both(3, high).astype(bf16), 2)
    to_y = jnp.concatenate([both(2, low) + diag_x.astype(f32), both(2, high)]).astype(bf16)
    to_x = jnp.concatenate([both(1, low), both(1, high) + diag_y.astype(f32)]).astype(bf16)
    from_y = flipped(to_y, 2)
    from_x = flipped(to_x, 1)
    mine = both(0) + from_x.astype(f32) + from_y.astype(f32)
    plane = lax.axis_index("dp") // 8
    buddy = quarter ^ 1
    near = (quarter // 2) ^ 1
    far = 2 * near + (0 if near > quarter // 2 else 1)
    step = plane_moved(mine.astype(bf16), [(buddy, quarter), (far ^ 1, far)])
    mine = mine + step.astype(f32)
    return mine + plane_moved(mine.astype(bf16), [(far, quarter)]).astype(f32)


def fast_device(tokens, params, lengths, cotangent):
    width = tokens.shape[1]
    hidden = FF
    f32, bf16 = jnp.float32, jnp.bfloat16
    whole = lax.all_gather(params, "dp", axis=0, tiled=True).reshape(-1, LANES)
    rows_all = whole.shape[0]
    parts = {}
    for quarter in range(QUARTERS):
        parts.update(unpack_quarter(whole, quarter, width, hidden))

    gain_one, shift_one = parts["norm1", 0][0], parts["norm1", 0][1]
    bias_q, bias_v = parts["bias_qv", 0][0], parts["bias_qv", 1][0]
    bias_out, gain_two, shift_two = (parts["norm2", 0][i] for i in range(3))
    bias_up = parts["bias_up", 0][0]
    bias_down = parts["bias_down", 0][0]
    w_qkv = parts["qkv", 0]
    w_out = parts["out", 0]
    ups = sorted(row for name, row in parts if name == "up")
    downs = sorted(row for name, row in parts if name == "down")
    w_ups = [(row, parts["up", row]) for row in ups]
    w_downs = [(row, parts["down", row]) for row in downs]

    seqs = lengths.shape[0]
    slots = tokens.shape[0] // seqs
    sequence_mask = attention_mask(lengths, slots)
    valid = row_valid(lengths, slots)
    residual = tokens.astype(f32)
    scaled, xhat_one, inverse_one = layer_norm_forward(residual, gain_one, shift_one)
    ln_one = scaled.astype(bf16)
    qkv_bias = jnp.concatenate([bias_q, jnp.zeros((width,), f32), bias_v])
    qkv = (matmul(ln_one, w_qkv) + qkv_bias).astype(bf16)
    queries = split_heads(qkv[:, :width], seqs, slots)
    key_rows = split_heads(qkv[:, width : 2 * width], seqs, slots)
    values = split_heads(qkv[:, 2 * width :], seqs, slots)
    scores = raw_scores(queries, key_rows, sequence_mask)
    peak = jnp.max(scores, axis=-1, keepdims=True)
    lse = peak + jnp.log(jnp.sum(jnp.exp(scores - peak), axis=-1, keepdims=True))
    probs_full = jnp.exp(scores - lse)
    probs = probs_full.astype(bf16)
    attn = batched("ghqk,gkhd->gqhd", probs, values).astype(bf16).reshape(-1, width)
    mid = residual + matmul(attn, w_out) + bias_out
    scaled, xhat_two, inverse_two = layer_norm_forward(mid, gain_two, shift_two)
    ln_two = scaled.astype(bf16)
    pre = bias_up
    for row, block in w_ups:
        pre = pre + matmul(ln_two[:, row : row + block.shape[0]], block)
    act = gelu(pre).astype(bf16)
    dout = valid * cotangent.astype(f32)
    dout_b = dout.astype(bf16)

    grads = {}
    dout_wide = lane_pad(dout_b)

    def grad_rows(left, right):
        return contract_rows(left, right).astype(bf16)

    for row, block in w_downs:
        grads["down", row] = grad_rows(act[:, row : row + block.shape[0]], dout_wide)
    grads["bias_down", 0] = vector_rows([jnp.sum(dout, axis=0)], 0)

    quarters = {}
    quarters[3] = reduce_quarter(*pack_quarter(grads, 3, width, hidden, rows_all), 3)

    out = mid + bias_down
    for row, block in w_downs:
        out = out + matmul(act[:, row : row + block.shape[0]], block)
    block_out = valid * out

    dact = jnp.concatenate([contract_cols(dout_b, block) for _, block in w_downs], axis=1)
    dpre = jax.vjp(gelu, pre)[1](dact)[0]
    dpre_b = dpre.astype(bf16)
    for row, block in w_ups:
        grads["up", row] = grad_rows(ln_two[:, row : row + block.shape[0]], dpre_b)
    grads["bias_up", 0] = vector_rows([jnp.sum(dpre, axis=0)], 0)
    quarters[2] = reduce_quarter(*pack_quarter(grads, 2, width, hidden, rows_all), 2)

    dln_two = jnp.concatenate([contract_cols(dpre_b, block) for _, block in w_ups], axis=1)
    dgain_two, dshift_two, normed_two = layer_norm_backward(dln_two, xhat_two, inverse_two, gain_two)
    dmid = dout + normed_two
    dmid_b = dmid.astype(bf16)
    grads["out", 0] = grad_rows(attn, lane_pad(dmid_b))
    grads["norm2", 0] = vector_rows([jnp.sum(dmid, axis=0), dgain_two, dshift_two], 0)
    dattn = contract_cols(dmid_b, w_out).astype(bf16)
    dattn_heads = split_heads(dattn, seqs, slots)
    dprobs = batched("gqhd,gkhd->ghqk", dattn_heads, values)
    dscores = probs_full * (dprobs - jnp.sum(probs_full * dprobs, axis=-1, keepdims=True))
    dscores_b = dscores.astype(bf16)
    factor = 1.0 / math.sqrt(HEAD)
    dquery = (batched("ghqk,gkhd->gqhd", dscores_b, key_rows) * factor).reshape(-1, width)
    dkey = (batched("ghqk,gqhd->gkhd", dscores_b, queries) * factor).reshape(-1, width)
    dvalue = batched("ghqk,gqhd->gkhd", probs, dattn_heads).reshape(-1, width)
    grads["bias_qv", 0] = vector_rows([jnp.sum(dquery, axis=0), jnp.sum(dvalue, axis=0)], 0)
    quarters[1] = reduce_quarter(*pack_quarter(grads, 1, width, hidden, rows_all), 1)

    dqkv = jnp.concatenate([dquery, dkey, dvalue], axis=1).astype(bf16)
    grads["qkv", 0] = grad_rows(ln_one, lane_pad(dqkv))
    dln_one = contract_cols(dqkv, w_qkv)
    dgain_one, dshift_one, normed_one = layer_norm_backward(dln_one, xhat_one, inverse_one, gain_one)
    grads["norm1", 0] = vector_rows([dgain_one, dshift_one], 0)
    quarters[0] = reduce_quarter(*pack_quarter(grads, 0, width, hidden, rows_all), 0)
    token_grad = dmid + normed_one

    plane = lax.axis_index("dp") // 8
    param_grad = quarters[0]
    for quarter in range(1, QUARTERS):
        param_grad = jnp.where(plane == quarter, quarters[quarter], param_grad)
    return (block_out, token_grad, param_grad.reshape(-1))


def per_device(tokens, params, lengths, cotangent):
    width = tokens.shape[1]
    devices = lax.axis_size("dp")
    if fits(width, FF, devices * params.shape[0], devices):
        return fast_device(tokens, params, lengths, cotangent)
    whole = lax.all_gather(params, "dp", axis=0, tiled=True)
    weights = unflatten(whole, width, FF)
    stored_forward_values, block_out = forward_pass(weights, tokens, lengths)
    token_grad, grads = backward_pass(weights, stored_forward_values, cotangent, lengths)
    flat = flatten_grads(grads, whole.shape[0])
    param_grad = owner_sum(flat, params.shape[0])
    return (block_out, token_grad, param_grad)


def solution(mesh):
    in_specs = (P("dp", None), P("dp"), P("dp"), P("dp", None))
    out_specs = (P("dp", None), P("dp", None), P("dp"))
    return jax.shard_map(
        per_device, mesh=mesh, in_specs=in_specs, out_specs=out_specs, check_vma=False
    )
```

```python
import math

import jax
import jax.numpy as jnp
from jax import lax
from jax.experimental import pallas as pl
from jax.experimental.pallas import tpu as pltpu
from jax.sharding import PartitionSpec as P

HEADS = 17
HEAD = 64
FF = 4352


EPS = 1e-05
NEGATIVE = -1e30
GELU_C = 0.7978845608028654


def swapped(block, axis, stride):
    count = lax.axis_size(axis)
    route = []
    for low in range(count):
        high = low | 1 << stride
        if high != low and high < count:
            route += [(low, high), (high, low)]
    return lax.ppermute(block, axis, route)


def param_shapes(width, hidden):
    return [
        (width,),
        (width,),
        (width, 3 * width),
        (width,),
        (width,),
        (width, width),
        (width,),
        (width,),
        (width,),
        (width, hidden),
        (hidden,),
        (hidden, width),
        (width,),
    ]


def unflatten(flat, width, hidden):
    pieces = []
    offset = 0
    for layout in param_shapes(width, hidden):
        extent = math.prod(layout)
        pieces.append(flat[offset : offset + extent].reshape(layout))
        offset += extent
    return pieces


def batched(form, left, right):
    return jnp.einsum(form, left, right, preferred_element_type=jnp.float32)


def matmul(left, right):
    return jnp.dot(left, right, preferred_element_type=jnp.float32)


def contract_rows(left, right):
    return lax.dot_general(
        left, right, (((0,), (0,)), ((), ())), preferred_element_type=jnp.float32
    )


def contract_cols(left, right):
    return lax.dot_general(
        left, right, (((1,), (1,)), ((), ())), preferred_element_type=jnp.float32
    )


def layer_norm_forward(rows, gain, shift):
    mean = jnp.mean(rows, axis=-1, keepdims=True)
    centred = rows - mean
    inverse = lax.rsqrt(jnp.mean(centred * centred, axis=-1, keepdims=True) + EPS)
    normed = centred * inverse
    return (normed * gain.astype(jnp.float32) + shift.astype(jnp.float32), normed, inverse)


def layer_norm_backward(upstream, normed, inverse, gain):
    dgain = jnp.sum(upstream * normed, axis=0)
    dshift = jnp.sum(upstream, axis=0)
    scaled = upstream * gain.astype(jnp.float32)
    inner = (
        scaled
        - jnp.mean(scaled, axis=-1, keepdims=True)
        - normed * jnp.mean(scaled * normed, axis=-1, keepdims=True)
    )
    return (dgain, dshift, inverse * inner)


def gelu(value):
    return 0.5 * value * (1.0 + jnp.tanh(GELU_C * (value + 0.044715 * value * value * value)))


def attention_mask(lengths, slots):
    position = jnp.arange(slots, dtype=jnp.int32)
    causal = position[:, None] >= position[None, :]
    inside = position[None, None, :] < lengths[:, None, None]
    return (causal[None, :, :] & inside)[:, None, :, :]


def row_valid(lengths, slots):
    position = jnp.arange(slots, dtype=jnp.int32)
    return (position[None, :] < lengths[:, None]).astype(jnp.float32).reshape(-1, 1)


def split_heads(block, seqs, slots):
    return block.reshape(seqs, slots, HEADS, HEAD)


def raw_scores(queries, key_rows, sequence_mask):
    scores = batched("gqhd,gkhd->ghqk", queries, key_rows) * (1.0 / math.sqrt(HEAD))
    return jnp.where(sequence_mask, scores, NEGATIVE)


def forward_pass(weights, tokens, lengths):
    (
        first_norm_gain,
        first_norm_shift,
        w_qkv,
        bias_q,
        bias_v,
        w_out,
        bias_out,
        second_norm_gain,
        second_norm_shift,
        w_up,
        bias_up,
        w_down,
        bias_down,
    ) = weights
    width = tokens.shape[1]
    seqs = lengths.shape[0]
    slots = tokens.shape[0] // seqs
    sequence_mask = attention_mask(lengths, slots)
    token_valid_mask = row_valid(lengths, slots)
    residual_stream = tokens.astype(jnp.float32)
    first_centred_scaled, first_standardized_input, first_inverse_deviation = layer_norm_forward(
        residual_stream, first_norm_gain, first_norm_shift
    )
    first_norm_output = first_centred_scaled.astype(jnp.bfloat16)
    qkv_bias = jnp.concatenate(
        [bias_q.astype(jnp.float32), jnp.zeros((width,), jnp.float32), bias_v.astype(jnp.float32)]
    )
    query_key_value = (matmul(first_norm_output, w_qkv) + qkv_bias).astype(jnp.bfloat16)
    queries = split_heads(query_key_value[:, :width], seqs, slots)
    key_rows = split_heads(query_key_value[:, width : 2 * width], seqs, slots)
    values = split_heads(query_key_value[:, 2 * width :], seqs, slots)
    scores = raw_scores(queries, key_rows, sequence_mask)
    peak = jnp.max(scores, axis=-1, keepdims=True)
    log_exp_totals = peak + jnp.log(jnp.sum(jnp.exp(scores - peak), axis=-1, keepdims=True))
    probs = jnp.exp(scores - log_exp_totals).astype(jnp.bfloat16)
    attention_result = (
        batched("ghqk,gkhd->gqhd", probs, values).astype(jnp.bfloat16).reshape(-1, width)
    )
    middle_residual = (
        residual_stream + matmul(attention_result, w_out) + bias_out.astype(jnp.float32)
    )
    second_centred_scaled, second_standardized_input, second_inverse_deviation = layer_norm_forward(
        middle_residual, second_norm_gain, second_norm_shift
    )
    second_norm_output = second_centred_scaled.astype(jnp.bfloat16)
    preactivation_values = matmul(second_norm_output, w_up) + bias_up.astype(jnp.float32)
    activation_values = gelu(preactivation_values).astype(jnp.bfloat16)
    block_out = token_valid_mask * (
        middle_residual + matmul(activation_values, w_down) + bias_down.astype(jnp.float32)
    )
    stored_forward_values = (
        token_valid_mask,
        sequence_mask,
        first_standardized_input,
        first_inverse_deviation,
        first_norm_output,
        query_key_value,
        log_exp_totals,
        attention_result,
        second_standardized_input,
        second_inverse_deviation,
        second_norm_output,
        preactivation_values,
        activation_values,
    )
    return (stored_forward_values, block_out)


def backward_pass(weights, stored_forward_values, cotangent, lengths):
    (
        first_norm_gain,
        first_norm_shift,
        w_qkv,
        bias_q,
        bias_v,
        w_out,
        bias_out,
        second_norm_gain,
        second_norm_shift,
        w_up,
        bias_up,
        w_down,
        bias_down,
    ) = weights
    (
        token_valid_mask,
        sequence_mask,
        first_standardized_input,
        first_inverse_deviation,
        first_norm_output,
        query_key_value,
        log_exp_totals,
        attention_result,
        second_standardized_input,
        second_inverse_deviation,
        second_norm_output,
        preactivation_values,
        activation_values,
    ) = stored_forward_values
    width = cotangent.shape[1]
    seqs = lengths.shape[0]
    slots = cotangent.shape[0] // seqs
    dout = token_valid_mask * cotangent.astype(jnp.float32)
    dout_b = dout.astype(jnp.bfloat16)
    grad_down = contract_rows(activation_values, dout_b)
    grad_bias_down = jnp.sum(dout, axis=0)
    dact = contract_cols(dout_b, w_down)
    dpre = jax.vjp(gelu, preactivation_values)[1](dact)[0]
    dpre_b = dpre.astype(jnp.bfloat16)
    grad_up = contract_rows(second_norm_output, dpre_b)
    grad_bias_up = jnp.sum(dpre, axis=0)
    second_norm_input_gradient = contract_cols(dpre_b, w_up)
    second_gain_gradient, second_shift_gradient, second_normed_gradient = layer_norm_backward(
        second_norm_input_gradient,
        second_standardized_input,
        second_inverse_deviation,
        second_norm_gain,
    )
    dmid = dout + second_normed_gradient
    dmid_b = dmid.astype(jnp.bfloat16)
    grad_out = contract_rows(attention_result, dmid_b)
    grad_bias_out = jnp.sum(dmid, axis=0)
    dattn = contract_cols(dmid_b, w_out).astype(jnp.bfloat16)
    queries = split_heads(query_key_value[:, :width], seqs, slots)
    key_rows = split_heads(query_key_value[:, width : 2 * width], seqs, slots)
    values = split_heads(query_key_value[:, 2 * width :], seqs, slots)
    scores = raw_scores(queries, key_rows, sequence_mask)
    probs_full = jnp.exp(scores - log_exp_totals)
    probs = probs_full.astype(jnp.bfloat16)
    dattn_heads = split_heads(dattn, seqs, slots)
    dprobs = batched("gqhd,gkhd->ghqk", dattn_heads, values)
    dscores = probs_full * (dprobs - jnp.sum(probs_full * dprobs, axis=-1, keepdims=True))
    dscores_b = dscores.astype(jnp.bfloat16)
    factor = 1.0 / math.sqrt(HEAD)
    dquery = (batched("ghqk,gkhd->gqhd", dscores_b, key_rows) * factor).reshape(-1, width)
    dkey = (batched("ghqk,gqhd->gkhd", dscores_b, queries) * factor).reshape(-1, width)
    dvalue = batched("ghqk,gqhd->gkhd", probs, dattn_heads).reshape(-1, width)
    grad_bias_q = jnp.sum(dquery, axis=0)
    grad_bias_v = jnp.sum(dvalue, axis=0)
    dqkv = jnp.concatenate([dquery, dkey, dvalue], axis=1).astype(jnp.bfloat16)
    grad_qkv = contract_rows(first_norm_output, dqkv)
    first_norm_input_gradient = contract_cols(dqkv, w_qkv)
    first_gain_gradient, first_shift_gradient, first_normed_gradient = layer_norm_backward(
        first_norm_input_gradient,
        first_standardized_input,
        first_inverse_deviation,
        first_norm_gain,
    )
    token_grad = dmid + first_normed_gradient
    grads = [
        first_gain_gradient,
        first_shift_gradient,
        grad_qkv,
        grad_bias_q,
        grad_bias_v,
        grad_out,
        grad_bias_out,
        second_gain_gradient,
        second_shift_gradient,
        grad_up,
        grad_bias_up,
        grad_down,
        grad_bias_down,
    ]
    return (token_grad, grads)


def flatten_grads(grads, padded_total):
    used = sum((math.prod(piece.shape) for piece in grads))
    tail = jnp.zeros((padded_total - used,), jnp.float32)
    return jnp.concatenate([piece.reshape(-1) for piece in grads] + [tail])


def owner_sum(flat, shard):
    levels = lax.axis_size("dp").bit_length() - 1
    current = flat.reshape((2,) * levels + (shard,))
    remaining = list(range(levels - 1, -1, -1))
    mine = lax.axis_index("dp")
    order = list(range(levels))
    for bit in order:
        where = remaining.index(bit)
        own_bit = mine >> bit & 1
        keep = lax.dynamic_index_in_dim(current, own_bit, where, keepdims=False)
        outgoing = lax.dynamic_index_in_dim(current, 1 - own_bit, where, keepdims=False)
        current = keep + swapped(outgoing, "dp", bit)
        remaining.pop(where)
    return current


LANES = 128
HALF = 64
TILE = 16
QUARTERS = 4
TAIL = 48
MARGIN = 1120
VMEM_BYTES = 60 * 1024 * 1024
COST = pl.CostEstimate(flops=10**7, transcendentals=0, bytes_accessed=6 * 10**7)


def pieces_of(width, hidden):
    short, wide, long = width // HALF, 3 * width // HALF, hidden // HALF
    table = {}
    at = 0
    for name, run, rows in (
        ("norm1", short, 2),
        ("qkv", wide, width),
        ("bias_qv", short, 2),
        ("out", short, width),
        ("norm2", short, 3),
        ("up", long, width),
        ("bias_up", long, 1),
        ("down", short, hidden),
        ("bias_down", short, 1),
    ):
        table[name] = (at, run, rows)
        at += run * rows
    return table


def quarter_plan(width, hidden, half_blocks):
    span = half_blocks // QUARTERS
    plan = [[] for _ in range(QUARTERS)]
    for name, (at, run, rows) in pieces_of(width, hidden).items():
        row = 0
        while row < rows:
            quarter = (at + (row + 1) * run - 1) // span
            last = min(rows, ((quarter + 1) * span - at) // run)
            plan[quarter].append((name, row, last - row))
            row = last
    return plan


def fits(width, hidden, total, devices):
    if devices != 32 or total % (LANES * TILE * devices) or width % HALF or hidden % HALF:
        return False
    for rows in quarter_plan(width, hidden, total // HALF):
        for name, _, count in rows:
            if name in ("qkv", "out", "up", "down") and count % TILE:
                return False
    return True


def unpack_quarter(slots, tail, quarter, width, hidden, rows_all):
    table = pieces_of(width, hidden)
    rows_q = rows_all // QUARTERS
    shard = rows_q // 8
    plan = quarter_plan(width, hidden, 2 * rows_all)[quarter]
    base = 2 * (quarter * rows_q - TAIL)
    matrices = ("qkv", "out", "up", "down")
    shapes = []
    for name, _, count in plan:
        run = table[name][1]
        if name in matrices:
            shapes.append(jax.ShapeDtypeStruct((count, run * HALF), jnp.bfloat16))
        else:
            shapes.append(jax.ShapeDtypeStruct((TILE, run * HALF), jnp.float32))
    shapes.append(jax.ShapeDtypeStruct((TAIL, LANES), jnp.bfloat16))
    choices = sorted(slots)

    def kernel(where_ref, tail_ref, *rest):
        srcs = rest[: 2 * len(choices)]
        outs = rest[2 * len(choices) : -3]
        flat, wide, sems = rest[-3:]
        me, chosen = where_ref[0], where_ref[1]

        def copies(pair):
            for i in range(8):
                to = jnp.bitwise_xor(me, i) * shard + TAIL
                yield pltpu.make_async_copy(
                    pair[i % 2].at[i // 2], flat.at[pl.ds(pl.multiple_of(to, TILE), shard)], sems.at[i]
                )

        for k, choice in enumerate(choices):

            @pl.when(chosen == choice)
            def _(k=k):
                for copy in copies(srcs[2 * k : 2 * k + 2]):
                    copy.start()

        flat[:TAIL] = tail_ref[...]
        for copy in copies(srcs[:2]):
            copy.wait()
        outs[-1][...] = flat[rows_q:]
        unroll = 37

        def spread(i, _):
            for u in range(unroll):
                step = i * unroll + u
                block = flat[pl.ds(pl.multiple_of(step * TILE, TILE), TILE), :].astype(jnp.float32)
                wide[pl.ds(2 * TILE * step, TILE, stride=2), :] = block
                wide[pl.ds(2 * TILE * step + 1, TILE, stride=2), :] = pltpu.roll(block, HALF, 1)
            return 0

        steps = (rows_q + TAIL) // TILE
        lax.fori_loop(0, steps // unroll, spread, 0)
        for step in range(steps // unroll * unroll, steps):
            block = flat[step * TILE : (step + 1) * TILE, :].astype(jnp.float32)
            wide[pl.ds(2 * TILE * step, TILE, stride=2), :] = block
            wide[pl.ds(2 * TILE * step + 1, TILE, stride=2), :] = pltpu.roll(block, HALF, 1)
        lane = lax.broadcasted_iota(jnp.int32, (TILE, LANES), 1)
        line = lax.broadcasted_iota(jnp.int32, (TILE, LANES), 0)
        for (name, row, count), out in zip(plan, outs):
            at, run, _ = table[name]
            start = at + row * run - base
            odd = (start + run * line) % 2 == 1
            swap = odd & (lane >= HALF)

            def group(g, _, out=out, run=run, start=start, swap=swap):
                begin = start + g * (TILE * run)
                where = pl.ds(pl.multiple_of(g * TILE, TILE), TILE)
                now = wide[pl.ds(begin, TILE, stride=run), :]
                for j in range((run + 1) // 2):
                    if 2 * j + 1 == run:
                        out[where, 2 * j * HALF : run * HALF] = now[:, :HALF].astype(out.dtype)
                        break
                    after = wide[pl.ds(begin + 2 * j + 2, TILE, stride=run), :]
                    value = jnp.where(swap, after, now)
                    out[where, 2 * j * HALF : 2 * j * HALF + LANES] = value.astype(out.dtype)
                    now = after
                return 0

            if name in matrices:
                lax.fori_loop(0, count // TILE, group, 0)
            else:
                group(0, 0)

    index = lax.axis_index("dp").astype(jnp.int32)
    plane = index // 8
    if quarter == 0:
        slot = jnp.where(plane == 0, 0, 1)
    elif quarter == QUARTERS - 1:
        slot = jnp.where(plane == quarter, 0, quarter)
    else:
        slot = jnp.where(plane == quarter, 0, jnp.where(plane > quarter, quarter + 1, quarter))
    where = jnp.stack([index % 8, slot])
    sources = [block for choice in choices for block in slots[choice]]
    *outs, tail = pl.pallas_call(
        kernel,
        out_shape=shapes,
        in_specs=[
            pl.BlockSpec(memory_space=pltpu.SMEM),
            pl.BlockSpec(memory_space=pltpu.VMEM),
        ]
        + [pl.BlockSpec(memory_space=pl.ANY)] * len(sources),
        out_specs=[pl.BlockSpec(memory_space=pltpu.VMEM)] * len(shapes),
        scratch_shapes=[
            pltpu.VMEM((rows_q + TAIL, LANES), jnp.bfloat16),
            pltpu.VMEM((2 * (rows_q + TAIL) + MARGIN, LANES), jnp.float32),
            pltpu.SemaphoreType.DMA((8,)),
        ],
        compiler_params=pltpu.CompilerParams(vmem_limit_bytes=VMEM_BYTES),
        cost_estimate=COST,
        name=f"unpack_{quarter}",
    )(where, tail, *sources)
    return {(name, row): out for (name, row, _), out in zip(plan, outs)}, tail


def lane_pad(block):
    return jnp.pad(block, ((0, 0), (0, -block.shape[1] % LANES)))


def vector_rows(rows, run):
    block = jnp.stack(rows).astype(jnp.bfloat16)
    return jnp.pad(block, ((0, TILE - len(rows)), (0, -block.shape[1] % LANES)))


def pack_quarter(grads, quarter, width, hidden, rows_all):
    table = pieces_of(width, hidden)
    rows_q = rows_all // QUARTERS
    shard = rows_q // 8
    base = 2 * rows_q * quarter
    span = 2 * rows_q
    shift = 2 * TAIL
    jobs = []
    for name, (at, run, rows) in table.items():
        for (key, first), block in grads.items():
            if key != name:
                continue
            count = block.shape[0] if name in ("qkv", "out", "up", "down") else TILE
            start = at + first * run - base
            if start >= span or start + min(count, rows) * run <= 0:
                continue
            if start + shift < 0:
                continue
            groups = min(count // TILE, -(-(span - start) // (TILE * run)))
            jobs.append((start + shift, run, groups, block[: groups * TILE]))
    jobs.sort(key=lambda job: job[0])

    def kernel(me_ref, *rest):
        ins = rest[: len(jobs)]
        keep, send = rest[len(jobs) : len(jobs) + 2]
        wide, flat, sems = rest[len(jobs) + 2 :]
        for (start, run, groups, _), src in zip(jobs, ins):

            def group(g, _, src=src, run=run, start=start):
                begin = start + g * (TILE * run)
                where = pl.ds(pl.multiple_of(g * TILE, TILE), TILE)
                for j in range((run + 1) // 2):
                    value = src[where, j * LANES : (j + 1) * LANES].astype(jnp.float32)
                    wide[pl.ds(begin + 2 * j, TILE, stride=run), :] = value
                    if 2 * j + 1 < run:
                        wide[pl.ds(begin + 2 * j + 1, TILE, stride=run), :] = pltpu.roll(value, HALF, 1)
                return 0

            lax.fori_loop(0, groups, group, 0)
        lane = lax.broadcasted_iota(jnp.int32, (TILE, LANES), 1)
        unroll = 31
        me = me_ref[0]
        for rel in range(8):
            where = jnp.bitwise_xor(me, rel) * shard

            def gather(i, _, where=where):
                for u in range(unroll):
                    line = pl.multiple_of(where + (i * unroll + u) * TILE, TILE)
                    low = wide[pl.ds(shift + 2 * line, TILE, stride=2), :]
                    high = wide[pl.ds(shift + 2 * line + 1, TILE, stride=2), :]
                    value = jnp.where(lane < HALF, low, pltpu.roll(high, HALF, 1))
                    flat[pl.ds(line, TILE), :] = value.astype(jnp.bfloat16)
                return 0

            lax.fori_loop(0, shard // TILE // unroll, gather, 0)
            target = send if rel % 2 else keep
            pltpu.make_async_copy(
                flat.at[pl.ds(pl.multiple_of(where, TILE), shard)], target.at[rel // 2], sems.at[rel]
            ).start()
        for rel in range(8):
            target = send if rel % 2 else keep
            pltpu.make_async_copy(
                flat.at[pl.ds(0, shard)], target.at[rel // 2], sems.at[rel]
            ).wait()

    me = (lax.axis_index("dp") % 8).astype(jnp.int32).reshape(1)
    out = jax.ShapeDtypeStruct((4, shard, LANES), jnp.bfloat16)
    return pl.pallas_call(
        kernel,
        out_shape=[out, out],
        in_specs=[pl.BlockSpec(memory_space=pltpu.SMEM)]
        + [pl.BlockSpec(memory_space=pltpu.VMEM)] * len(jobs),
        out_specs=[pl.BlockSpec(memory_space=pl.ANY)] * 2,
        scratch_shapes=[
            pltpu.VMEM((shift + span + MARGIN, LANES), jnp.float32),
            pltpu.VMEM((rows_q, LANES), jnp.bfloat16),
            pltpu.SemaphoreType.DMA((8,)),
        ],
        compiler_params=pltpu.CompilerParams(vmem_limit_bytes=VMEM_BYTES),
        cost_estimate=COST,
        name=f"pack_{quarter}",
    )(me, *[job[3] for job in jobs])


def flipped(block, bit):
    return swapped(block, "dp", bit)


def plane_moved(block, moves):
    route = [(8 * a + i, 8 * b + i) for a, b in moves for i in range(8)]
    return lax.ppermute(block, "dp", route)


class Reduction:
    def __init__(self, quarter):
        self.quarter = quarter

    def core(self, keep, send):
        self.keep = keep
        self.other = flipped(send, 0)
        return self.other

    def both(self, i, rows=slice(None)):
        return self.keep[i, rows].astype(jnp.float32) + self.other[i, rows].astype(jnp.float32)

    def diagonal(self, other):
        self.other = other
        cut = self.keep.shape[1] // 2 // TILE * TILE
        self.low, self.high = slice(0, cut), slice(cut, None)
        self.diag = (
            flipped(self.both(3, self.low).astype(jnp.bfloat16), 1),
            flipped(self.both(3, self.high).astype(jnp.bfloat16), 2),
        )
        return self.diag

    def sides(self, diag):
        f32, bf16 = jnp.float32, jnp.bfloat16
        low, high = self.low, self.high
        to_y = jnp.concatenate([self.both(2, low) + diag[0].astype(f32), self.both(2, high)])
        to_x = jnp.concatenate([self.both(1, low), self.both(1, high) + diag[1].astype(f32)])
        return flipped(to_x.astype(bf16), 1), flipped(to_y.astype(bf16), 2)

    def near(self, sides):
        quarter = self.quarter
        mine = self.both(0) + sides[0].astype(jnp.float32) + sides[1].astype(jnp.float32)
        other = (quarter // 2) ^ 1
        self.relay = 2 * other + (0 if other > quarter // 2 else 1)
        self.mine = mine
        return plane_moved(
            mine.astype(jnp.bfloat16), [(quarter ^ 1, quarter), (self.relay ^ 1, self.relay)]
        )

    def far(self, step):
        self.mine = self.mine + step.astype(jnp.float32)
        return plane_moved(self.mine.astype(jnp.bfloat16), [(self.relay, self.quarter)])

    def total(self, step):
        return self.mine + step.astype(jnp.float32)


def fence(*values):
    return lax.optimization_barrier(values)


class Gathering:
    def __init__(self, unit):
        self.unit = unit
        self.cut = unit.shape[0] // 2 // TILE * TILE

    def sides(self):
        return flipped(self.unit, 1), flipped(self.unit, 2)

    def diagonal(self, sides):
        self.near = sides
        return flipped(sides[1][: self.cut], 1), flipped(sides[0][self.cut :], 2)

    def core(self, diagonal):
        mine = jnp.concatenate([self.unit, *self.near, *diagonal]).reshape(4, *self.unit.shape)
        return mine, flipped(mine, 0)


def fast_device(tokens, params, lengths, cotangent):
    width = tokens.shape[1]
    hidden = FF
    f32, bf16 = jnp.float32, jnp.bfloat16
    own = params.reshape(-1, LANES)
    rows_all = own.shape[0] * lax.axis_size("dp")
    plane = lax.axis_index("dp") // 8
    inner = (plane == 1) | (plane == 2)
    even = plane % 2 == 0
    parts = {}
    slots = {}

    def unpacked(quarter, choices, tail):
        return unpack_quarter(
            {choice: slots[choice] for choice in choices}, tail, quarter, width, hidden, rows_all
        )

    slot0 = Gathering(own)
    first = plane_moved(own, [(0, 2), (1, 0), (3, 1), (2, 3)])
    sides0 = slot0.sides()
    first, sides0 = fence(first, sides0)
    second = plane_moved(jnp.where(inner, first, own), [(0, 1), (2, 3), (3, 2), (1, 0)])
    third = plane_moved(own, [(2, 1), (1, 2)])
    diag0 = slot0.diagonal(sides0)
    seqs = lengths.shape[0]
    slots_each = tokens.shape[0] // seqs
    sequence_mask = attention_mask(lengths, slots_each)
    valid = row_valid(lengths, slots_each)
    residual = tokens.astype(f32)
    second, third, diag0 = fence(second, third, diag0)

    slot1 = Gathering(jnp.where(even, first, second))
    sides1 = slot1.sides()
    fourth = plane_moved(third, [(1, 0), (2, 3)])
    slots[0] = slot0.core(diag0)
    sides1, fourth, slots[0] = fence(sides1, fourth, slots[0])

    diag1 = lax.optimization_barrier(slot1.diagonal(sides1))

    slot2 = Gathering(jnp.where(inner, third, fourth))
    sides2 = slot2.sides()
    slots[1] = slot1.core(diag1)
    sides2, unpack = fence(sides2, unpacked(0, (0, 1), jnp.zeros((TAIL, LANES), bf16)))
    parts.update(unpack[0])

    diag2 = slot2.diagonal(sides2)
    gain_one, shift_one = parts["norm1", 0][0], parts["norm1", 0][1]
    w_qkv = parts["qkv", 0]
    bias_q = parts["bias_qv", 0][0]
    scaled, xhat_one, inverse_one = layer_norm_forward(residual, gain_one, shift_one)
    ln_one = scaled.astype(bf16)
    qkv = matmul(ln_one, w_qkv)
    diag2, qkv, ln_one, xhat_one, inverse_one = fence(diag2, qkv, ln_one, xhat_one, inverse_one)

    slot3 = Gathering(jnp.where(even, second, first))
    sides3 = slot3.sides()
    slots[2] = slot2.core(diag2)
    queries = split_heads((qkv[:, :width] + bias_q).astype(bf16), seqs, slots_each)
    key_rows = split_heads(qkv[:, width : 2 * width].astype(bf16), seqs, slots_each)
    scores = raw_scores(queries, key_rows, sequence_mask)
    peak = jnp.max(scores, axis=-1, keepdims=True)
    lse = peak + jnp.log(jnp.sum(jnp.exp(scores - peak), axis=-1, keepdims=True))
    probs_full = jnp.exp(scores - lse)
    sides3, probs_full, unpack = fence(sides3, probs_full, unpacked(1, (0, 1, 2), unpack[1]))
    parts.update(unpack[0])

    diag3 = slot3.diagonal(sides3)
    bias_v = parts["bias_qv", 1][0]
    bias_out, gain_two, shift_two = (parts["norm2", 0][i] for i in range(3))
    w_out = parts["out", 0]
    values = split_heads((qkv[:, 2 * width :] + bias_v).astype(bf16), seqs, slots_each)
    probs = probs_full.astype(bf16)
    attn = batched("ghqk,gkhd->gqhd", probs, values).astype(bf16).reshape(-1, width)
    diag3, attn = fence(diag3, attn)

    slots[3] = slot3.core(diag3)
    mid = residual + matmul(attn, w_out) + bias_out
    scaled, xhat_two, inverse_two = layer_norm_forward(mid, gain_two, shift_two)
    ln_two = scaled.astype(bf16)
    w_up0 = parts["up", 0]
    pre = matmul(ln_two[:, : w_up0.shape[0]], w_up0)
    slots[3], mid, ln_two, pre, xhat_two, inverse_two = fence(
        slots[3], mid, ln_two, pre, xhat_two, inverse_two
    )

    found, tail = unpacked(2, (0, 2, 3), unpack[1])
    parts.update(found)
    bias_up = parts["bias_up", 0][0]
    ups = sorted(row for name, row in parts if name == "up")
    w_ups = [(row, parts["up", row]) for row in ups]
    pre = pre + bias_up
    for row, block in w_ups[1:]:
        pre = pre + matmul(ln_two[:, row : row + block.shape[0]], block)
    act = gelu(pre).astype(bf16)
    dout = valid * cotangent.astype(f32)
    dout_b = dout.astype(bf16)

    grads = {}
    plan_rows = quarter_plan(width, hidden, 2 * rows_all)
    dout_wide = lane_pad(dout_b)

    def grad_rows(left, right):
        return contract_rows(left, right).astype(bf16)

    starts = [row for q in plan_rows for name, row, _ in q if name == "down"] + [hidden]
    for row, after in zip(starts, starts[1:]):
        grads["down", row] = grad_rows(act[:, row:after], dout_wide)
    grads["bias_down", 0] = vector_rows([jnp.sum(dout, axis=0)], 0)

    red = [Reduction(quarter) for quarter in range(QUARTERS)]

    def packed(quarter):
        return pack_quarter(grads, quarter, width, hidden, rows_all)

    pack, mid, act, dout_b = fence(packed(3), mid, act, dout_b)
    core3 = red[3].core(*pack)
    parts.update(unpacked(3, (0, 3), tail)[0])
    bias_down = parts["bias_down", 0][0]
    downs = sorted(row for name, row in parts if name == "down")
    w_downs = [(row, parts["down", row]) for row in downs]
    dact = jnp.concatenate([contract_cols(dout_b, block) for _, block in w_downs], axis=1)
    dpre = jax.vjp(gelu, pre)[1](dact)[0]
    dpre_b = dpre.astype(bf16)
    core3, dpre, dpre_b = fence(core3, dpre, dpre_b)

    diag3 = red[3].diagonal(core3)
    for row, block in w_ups:
        grads["up", row] = grad_rows(ln_two[:, row : row + block.shape[0]], dpre_b)
    grads["bias_up", 0] = vector_rows([jnp.sum(dpre, axis=0)], 0)
    out = mid + bias_down
    for row, block in w_downs:
        out = out + matmul(act[:, row : row + block.shape[0]], block)
    block_out = valid * out
    diag3, ups_done, bias_done, block_out = fence(
        diag3, [grads["up", row] for row in ups], grads["bias_up", 0], block_out
    )
    for row, block in zip(ups, ups_done):
        grads["up", row] = block
    grads["bias_up", 0] = bias_done

    sides3 = red[3].sides(diag3)
    sides3, pack, dpre_b = fence(sides3, packed(2), dpre_b)

    core2 = red[2].core(*pack)
    near3 = red[3].near(sides3)
    dln_two = jnp.concatenate([contract_cols(dpre_b, block) for _, block in w_ups], axis=1)
    dgain_two, dshift_two, normed_two = layer_norm_backward(dln_two, xhat_two, inverse_two, gain_two)
    dmid = dout + normed_two
    dmid_b = dmid.astype(bf16)
    dattn = contract_cols(dmid_b, w_out).astype(bf16)
    core2, dattn, dmid, dmid_b, dgain_two, dshift_two = fence(
        core2, dattn, dmid, dmid_b, dgain_two, dshift_two
    )

    diag2 = red[2].diagonal(core2)
    dattn_heads = split_heads(dattn, seqs, slots_each)
    dprobs = batched("gqhd,gkhd->ghqk", dattn_heads, values)
    dscores = probs_full * (dprobs - jnp.sum(probs_full * dprobs, axis=-1, keepdims=True))
    dscores_b = dscores.astype(bf16)
    factor = 1.0 / math.sqrt(HEAD)
    dquery = (batched("ghqk,gkhd->gqhd", dscores_b, key_rows) * factor).reshape(-1, width)
    dkey = (batched("ghqk,gqhd->gkhd", dscores_b, queries) * factor).reshape(-1, width)
    dvalue = batched("ghqk,gqhd->gkhd", probs, dattn_heads).reshape(-1, width)
    grads["out", 0] = grad_rows(attn, lane_pad(dmid_b))
    grads["norm2", 0] = vector_rows([jnp.sum(dmid, axis=0), dgain_two, dshift_two], 0)
    grads["bias_qv", 0] = vector_rows([jnp.sum(dquery, axis=0), jnp.sum(dvalue, axis=0)], 0)
    dqkv = jnp.concatenate([dquery, dkey, dvalue], axis=1).astype(bf16)
    diag2, near3, dqkv, grads["out", 0], grads["norm2", 0], grads["bias_qv", 0] = fence(
        diag2, near3, dqkv, grads["out", 0], grads["norm2", 0], grads["bias_qv", 0]
    )

    sides2 = red[2].sides(diag2)
    far3 = red[3].far(near3)
    sides2, pack, dqkv = fence(sides2, packed(1), dqkv)

    core1 = red[1].core(*pack)
    near2 = red[2].near(sides2)
    grads["qkv", 0] = grad_rows(ln_one, lane_pad(dqkv))
    core1, far3, grads["qkv", 0], dqkv = fence(core1, far3, grads["qkv", 0], dqkv)

    diag1 = red[1].diagonal(core1)
    dln_one = contract_cols(dqkv, w_qkv)
    dgain_one, dshift_one, normed_one = layer_norm_backward(dln_one, xhat_one, inverse_one, gain_one)
    grads["norm1", 0] = vector_rows([dgain_one, dshift_one], 0)
    token_grad = dmid + normed_one
    diag1, near2, grads["norm1", 0], token_grad = fence(diag1, near2, grads["norm1", 0], token_grad)

    sides1 = red[1].sides(diag1)
    far2 = red[2].far(near2)
    sides1, pack = fence(sides1, packed(0))

    core0 = red[0].core(*pack)
    near1 = red[1].near(sides1)
    core0, far2 = fence(core0, far2)
    diag0 = red[0].diagonal(core0)
    diag0, near1 = fence(diag0, near1)
    sides0 = red[0].sides(diag0)
    far1 = red[1].far(near1)
    others = jnp.where(plane == 3, red[3].total(far3), red[2].total(far2))
    sides0, far1, others = fence(sides0, far1, others)
    near0 = red[0].near(sides0)
    others = jnp.where(plane == 1, red[1].total(far1), others)
    near0, others = fence(near0, others)
    far0 = red[0].far(near0)
    param_grad = jnp.where(plane == 0, red[0].total(far0), others)
    return (block_out, token_grad, param_grad.reshape(-1))


def per_device(tokens, params, lengths, cotangent):
    width = tokens.shape[1]
    devices = lax.axis_size("dp")
    if fits(width, FF, devices * params.shape[0], devices):
        return fast_device(tokens, params, lengths, cotangent)
    whole = lax.all_gather(params, "dp", axis=0, tiled=True)
    weights = unflatten(whole, width, FF)
    stored_forward_values, block_out = forward_pass(weights, tokens, lengths)
    token_grad, grads = backward_pass(weights, stored_forward_values, cotangent, lengths)
    flat = flatten_grads(grads, whole.shape[0])
    param_grad = owner_sum(flat, params.shape[0])
    return (block_out, token_grad, param_grad)


def solution(mesh):
    in_specs = (P("dp", None), P("dp"), P("dp"), P("dp", None))
    out_specs = (P("dp", None), P("dp", None), P("dp"))
    return jax.shard_map(
        per_device, mesh=mesh, in_specs=in_specs, out_specs=out_specs, check_vma=False
    )
```
